32 devices in a mesh: groups: 2 (over x), slab: 16 (over z, y, core).
Axes of the slice: x: 2, y: 2, z: 4, core: 2. Of those that a mesh axis runs over, the one named last changes fastest.
Arguments:
- wave_now: float32 [4, 16, 32, 8, 1024], P('groups', 'slab'), parts along dimension 0, may hold values from -6 to 6
- wave_prev: float32 [4, 16, 32, 8, 1024], P('groups', 'slab'), parts along dimension 0, may hold values from -6 to 6
- potential: float32 [16, 32, 8, 1024], P('slab'), may hold values from -1.5 to 1.5
- angular_dvr: float32 [1024, 1024], replicated, may hold values from -0.1875 to 0.1875
- kinetic_radial: float32 [16, 16], replicated, may hold values from -1.5 to 1.5
- kinetic_bond: float32 [32, 32], replicated, may hold values from -1 to 1
- kinetic_third: float32 [8, 8], replicated, may hold values from -2 to 2
- inv_moment: float32 [16], P('slab'), may hold values from 0.2 to 2
- rot_level: float32 [1024], replicated, may hold values from 0.1 to 2
- helicity: float32 [2], replicated, may hold values from 0 to 1.5
- coriolis: float32 [1], replicated, may hold values from 0.5 to 1.5
- ladder: float32 [1024], replicated, may hold values from 0.2 to 1.5
- damping: float32 [16, 32, 8], P('slab'), may hold values from 0.5 to 1
- strip_bond: int32 [16, 128], P('slab'), may hold values from 0 to 28
- strip_third: int32 [16, 128], P('slab'), may hold values from 0 to 7
- strip_weight: float32 [16, 128, 4], P('slab'), may hold values from -3 to 3
- strip_length: int32 [16], P('slab'), may hold values from 1 to 128, 1843 in all
- strip_owner: int32 [16, 128, 1], P('slab'), may hold values from 0 to 15; in each aligned block of 128 rows (0 to 127, 128 to 255, ..., all dimensions but the last counted through in order) at most 16 rows name the same one
- strip_cell: int32 [16, 128], P('slab'), may hold values from 0 to 63
Outputs:
- wave_next: float32 [4, 16, 32, 8, 1024], P('groups', 'slab'), parts along dimension 0
- surface_flux: float32 [4, 1024, 1024], P('groups', 'slab'), parts along dimension 0
The draws below stay inside these ranges and needn't reach their ends.
There are 2 independent parts, one for each index of `groups`. The reference program is written for one: setup_inputs(seed, part) draws one part's arguments, and reference() takes and returns one part's arrays. A program takes and returns all parts, laid end to end along the dimension named above; an argument that names none is the same for every part. Nothing has to cross between parts.
Inputs may be any that keep to these rules, and one draw needn't show every extreme that they name: `strip_owner`: among the 128 points of one R index, at most 16 name the same owner, and in every draw some owner is named by exactly 16 of them. `strip_length`: some R index has all 128 points live in every draw.
All inputs are finite; a program needn't handle non-finite values. No bound on the sum of `strip_length` on one device may be relied on, other than what follows from the above.
Results may differ from the reference program's by a relative error of at most 0.0003.
Values sent between devices are 32-bit elements; how exact they have to be, the bound alone decides.
A program may use at most 128 MiB of HBM per device.

```python
import math
import jax
import jax.numpy as jnp
import numpy as np
from jax import lax

K = 2
NRR = 32
NZ = 8
NA = 1024
SMAX = 128
P_DEV = 64
NR = 16
CAP = 16
NPROD = 1024
N_SLAB = 16


def touch_ends(drawn, stream_key, least, high):
    extent = drawn.shape
    place = [jax.random.randint(jax.random.fold_in(stream_key, axis), (), 0, extent[axis]) for axis in range(len(extent))]
    drawn = drawn.at[tuple(place)].set(least)
    longest = extent.index(max(extent))
    place[longest] = (place[longest] + 1) % extent[longest]
    return drawn.at[tuple(place)].set(high)


def block_scale(own_key, shape, split, low, high):
    level, own = 1.0, jax.random.fold_in(own_key, 6)
    for dim, shards_of in split:
        steps = jnp.exp(jax.random.uniform(jax.random.fold_in(own, dim), (shards_of,), jnp.float32, low / len(split), high / len(split)))
        level = level * jnp.repeat(steps, shape[dim] // shards_of).reshape([-1 if axis == dim else 1 for axis in range(len(shape))])
    return level


def profile(amount, total, reach, slope):
    weights = [(1 << 20) // math.isqrt(standing ** slope) + 1 for standing in range(2, amount + 1)]
    spare, given = total - reach - (amount - 1), [1] * (amount - 1)
    while spare > 0:
        movable = [i for i in range(amount - 1) if given[i] < reach]
        mass, left = sum([weights[i] for i in movable]), spare
        for i in movable:
            addition = min(reach - given[i], max(1, left * weights[i] // mass), spare)
            given[i] = given[i] + addition
            spare = spare - addition
    return np.array([reach] + given)


def uneven_parts(key, number_of, total, reach, slope):
    if number_of == 2:
        one = jax.random.randint(key, (), max(1, total - reach), min(reach, total - 1) + 1)
        return jnp.stack([one, total - one])
    tallies = jnp.asarray(profile(number_of, total, reach, slope), jnp.int32)
    pairs = (number_of - 1) // 2
    source_of, taker = tallies[1:1 + 2 * pairs:2], tallies[2:2 + 2 * pairs:2]
    room = jnp.minimum(source_of - 1, reach - taker)
    shifted = jax.random.randint(jax.random.fold_in(key, 1), (pairs,), 0, 1 << 20) % (room + 1)
    tallies = tallies.at[1:1 + 2 * pairs:2].set(source_of - shifted).at[2:2 + 2 * pairs:2].set(taker + shifted)
    return tallies[jax.random.permutation(jax.random.fold_in(key, 2), number_of)]


def shared_out(stream_key, own, number, rows, count, top, most, slope):
    sequence = jax.random.permutation(stream_key, count)
    heavy_load, ordinary = portions_of(count, rows * top, most, slope, True), portions_of(count, rows * top, most, slope, False)
    places = jnp.arange(count)

    def named(sizes, rotation):
        used = int((sizes > 0).sum())
        fixed = max(1, used // 4)
        shifted = fixed + (places - fixed + rotation * (used - fixed)) % max(1, count - fixed)
        return jnp.zeros((count,), jnp.int32).at[sequence[jnp.where(places < fixed, places, shifted)]].set(jnp.asarray(sizes, jnp.int32))

    sizes = jnp.where(number % 4 == 0, named(heavy_load, number // 4), named(ordinary, number - number // 4 - 1))
    mixed = jax.random.permutation(jax.random.fold_in(own, 3), count)
    source_of, taker = mixed[0:count // 2 * 2:2], mixed[1:count // 2 * 2:2]
    slack = jnp.minimum(sizes[source_of] - 1, most - sizes[taker]) // 2
    slack = jnp.where((source_of == sequence[0]) | (taker == sequence[0]) | (sizes[taker] == 0), 0, jnp.maximum(slack, 0))
    shifted = jax.random.randint(jax.random.fold_in(own, 4), (count // 2,), 0, 1 << 20) % (slack + 1)
    sizes = sizes.at[source_of].add(-shifted).at[taker].add(shifted)
    members = jnp.searchsorted(jnp.cumsum(sizes), jnp.arange(rows * top), side="right").astype(jnp.int32)
    listing = members.reshape(top, rows).T
    listing = listing[jax.random.permutation(jax.random.fold_in(own, 1), rows)]
    rotation = jax.random.randint(jax.random.fold_in(own, 2), (rows, 1), 0, top)
    return jnp.take_along_axis(listing, (jnp.arange(top)[None, :] + rotation) % top, axis=1)


def portions_of(count, total, most, lean, full):
    weights = [(1 << 20) // math.isqrt(rank ** lean) + 1 for rank in range(1, count + 1)]
    largest = most if full else min(most, max(-(-total // count), total * weights[0] // sum(weights)))
    least = 1 if total - largest >= count - 1 else 0
    given, surplus = [largest] + [least] * (count - 1), total - largest - least * (count - 1)
    while surplus > 0:
        movable = [i for i in range(1, count) if given[i] < largest] or [i for i in range(1, count) if given[i] < most]
        pool, left = sum([weights[i] for i in movable]), surplus
        for i in movable:
            addition = min(most - given[i], max(1, left * weights[i] // pool), surplus)
            given[i] = given[i] + addition
            surplus = surplus - addition
    return np.array(given)


def noise(stream_key, shape, width, limit, pieces=(), kind=jnp.bfloat16):
    gain = block_scale(stream_key, shape, pieces, -0.22, 0.18) if pieces else 1.0
    values = jax.random.normal(stream_key, shape, jnp.float32) * width * gain
    return jnp.minimum(jnp.maximum(values, -limit), limit).astype(kind)


def setup_inputs(seed: int = 0, part: int = 0) -> dict:
    key_of = jax.random.split(jax.random.key(seed), 20)
    part_splits = jax.random.split(jax.random.fold_in(key_of[19], part), 20)
    wave_now = noise(part_splits[0], (K, NR, NRR, NZ, NA), 1.0, 6.0, ((1, 16),), jnp.float32)
    wave_prev = noise(part_splits[1], (K, NR, NRR, NZ, NA), 1.0, 6.0, ((1, 16),), jnp.float32)
    potential = jnp.clip(jax.random.uniform(key_of[2], (NR, NRR, NZ, NA), jnp.float32, -1.5, 1.5) * block_scale(key_of[2], (NR, NRR, NZ, NA), ((0, 16),), -0.4, 0.0), -1.5, 1.5)
    angular_dvr = noise(key_of[3], (NA, NA), NA ** -0.5, 0.1875, (), jnp.float32)
    kinetic_radial = noise(key_of[4], (NR, NR), NR ** -0.5, 1.5, (), jnp.float32)
    kinetic_bond = noise(key_of[5], (NRR, NRR), NRR ** -0.5, 1.0, (), jnp.float32)
    kinetic_third = noise(key_of[6], (NZ, NZ), NZ ** -0.5, 2.0, (), jnp.float32)
    inv_moment = jnp.clip(jnp.exp(math.log(2.0) - 2.3025851 * jax.random.uniform(key_of[7], (NR,), jnp.float32) ** block_scale(key_of[7], (NR,), ((0, 16),), -0.2, 0.2)), 0.2, 2.0)
    rot_level = jnp.clip(jnp.exp(jax.random.uniform(key_of[8], (NA,), jnp.float32, math.log(0.1), math.log(2.0))), 0.1, 2.0)
    helicity = jnp.clip(jax.random.uniform(key_of[9], (K,), jnp.float32, 0.0, 1.5), 0.0, 1.5)
    coriolis = jnp.clip(jax.random.uniform(key_of[10], (K - 1,), jnp.float32, 0.5, 1.5), 0.5, 1.5)
    ladder = jnp.clip(jax.random.uniform(key_of[11], (NA,), jnp.float32, 0.2, 1.5), 0.2, 1.5)
    damping = jnp.clip(0.5 + 0.5 * jax.random.uniform(key_of[12], (NR, NRR, NZ), jnp.float32) ** block_scale(key_of[12], (NR, NRR, NZ), ((0, 16),), -0.2, 0.2), 0.5, 1.0)
    strip_bond = touch_ends(jax.random.randint(key_of[13], (NR, SMAX), 0, NRR - 3), jax.random.fold_in(key_of[13], 1), 0, (NRR - 3) - 1).astype(jnp.int32)
    strip_third = touch_ends(jax.random.randint(key_of[14], (NR, SMAX), 0, NZ), jax.random.fold_in(key_of[14], 1), 0, NZ - 1).astype(jnp.int32)
    strip_weight = noise(key_of[15], (NR, SMAX, 4), 0.5, 3.0, ((0, 16),), jnp.float32)
    strip_length = uneven_parts(key_of[16], NR, (NR * SMAX * 9) // 10, SMAX, 2).astype(jnp.int32)
    strip_owner_keys = jax.random.split(jax.random.fold_in(key_of[17], 1), NR * SMAX // SMAX)
    strip_owner_turns = jax.random.permutation(jax.random.fold_in(key_of[17], 3), NR * SMAX // SMAX)
    strip_owner = jax.vmap(lambda own, number: shared_out(jax.random.fold_in(key_of[17], 2), own, number, SMAX, N_SLAB, 1, CAP, 2))(strip_owner_keys, strip_owner_turns).reshape((NR, SMAX, 1))
    strip_cell = touch_ends(jax.random.randint(key_of[18], (NR, SMAX), 0, P_DEV), jax.random.fold_in(key_of[18], 1), 0, P_DEV - 1).astype(jnp.int32)
    return dict(wave_now=wave_now, wave_prev=wave_prev, potential=potential, angular_dvr=angular_dvr, kinetic_radial=kinetic_radial, kinetic_bond=kinetic_bond, kinetic_third=kinetic_third, inv_moment=inv_moment, rot_level=rot_level, helicity=helicity, coriolis=coriolis, ladder=ladder, damping=damping, strip_bond=strip_bond, strip_third=strip_third, strip_weight=strip_weight, strip_length=strip_length, strip_owner=strip_owner, strip_cell=strip_cell)


exact_prec = lax.Precision.HIGHEST


def hamiltonian_apply(wave, radial_term, potential, angular_dvr, kinetic_bond, kinetic_third, inv_moment, rot_level, helicity, coriolis, ladder):
    bond_term = jnp.einsum("ij,kqjza->kqiza", kinetic_bond, wave, precision=exact_prec)
    third_term = jnp.einsum("ij,kqrja->kqria", kinetic_third, wave, precision=exact_prec)
    grid_wave = jnp.einsum("kqrzb,ba->kqrza", wave, angular_dvr, precision=exact_prec)
    potential_term = jnp.einsum("kqrza,ba->kqrzb", potential[None] * grid_wave, angular_dvr, precision=exact_prec)
    moment = inv_moment[None, :, None, None, None]
    rotation_term = moment * (rot_level[None, None, None, None, :] + helicity[:, None, None, None, None]) * wave
    padding = jnp.zeros((1,) + wave.shape[1:], jnp.float32)
    couple = coriolis[:, None, None, None, None]
    above = jnp.concatenate([wave[1:] * couple, padding], axis=0)
    below = jnp.concatenate([padding, wave[:-1] * couple], axis=0)
    coriolis_term = moment * ladder[None, None, None, None, :] * (above + below)
    return radial_term + bond_term + third_term + potential_term + rotation_term + coriolis_term


def reference(wave_now, wave_prev, potential, angular_dvr, kinetic_radial, kinetic_bond, kinetic_third, inv_moment, rot_level, helicity, coriolis, ladder, damping, strip_bond, strip_third, strip_weight, strip_length, strip_owner, strip_cell):
    radial_term = jnp.einsum("ij,kjrza->kirza", kinetic_radial, wave_now, precision=exact_prec)
    hamiltonian = hamiltonian_apply(wave_now, radial_term, potential, angular_dvr, kinetic_bond, kinetic_third, inv_moment, rot_level, helicity, coriolis, ladder)
    damp = damping[None, :, :, :, None]
    wave_next = damp * (0.5 * hamiltonian - damp * wave_prev)

    by_slab = jnp.transpose(wave_now.reshape(K, NR, NRR * NZ, NA), (1, 0, 2, 3))
    stencil_step = jnp.arange(4, dtype=jnp.int32)

    def one_slab(inputs):
        cells, bond_pts, third_pts, weights, length = inputs
        cell_idx = ((bond_pts[:, None] + stencil_step[None, :]) * NZ + third_pts[:, None]).astype(jnp.int32)
        stencil = jnp.take(cells, cell_idx.reshape(-1), axis=1).reshape(K, SMAX, 4, NA)
        surface = jnp.einsum("st,ksta->ksa", weights, stencil, precision=exact_prec)
        alive_mask = (jnp.arange(SMAX, dtype=jnp.int32) < length).astype(jnp.float32)
        return jnp.transpose(surface * alive_mask[None, :, None], (1, 0, 2))

    surfaces = lax.map(one_slab, (by_slab, strip_bond, strip_third, strip_weight, strip_length))
    target = (strip_owner[:, :, 0] * P_DEV + strip_cell).astype(jnp.int32).reshape(-1)
    summed = jax.ops.segment_sum(surfaces.reshape(NR * SMAX, K, NA), target, num_segments=NPROD)
    surface_flux = jnp.transpose(summed, (1, 0, 2))
    return wave_next, surface_flux
```

```python
import jax
import jax.numpy as jnp
from jax import lax
from jax.sharding import PartitionSpec as P

SMAX = 128
P_DEV = 64


exact_prec = lax.Precision.HIGHEST


def hamiltonian_apply(
    wave,
    radial_term,
    potential,
    angular_dvr,
    kinetic_bond,
    kinetic_third,
    inv_moment,
    rot_level,
    helicity,
    coriolis,
    ladder,
):
    bond_term = jnp.einsum("ij,kqjza->kqiza", kinetic_bond, wave, precision=exact_prec)
    third_term = jnp.einsum("ij,kqrja->kqria", kinetic_third, wave, precision=exact_prec)
    grid_wave = jnp.einsum("kqrzb,ba->kqrza", wave, angular_dvr, precision=exact_prec)
    potential_term = jnp.einsum(
        "kqrza,ba->kqrzb", potential[None] * grid_wave, angular_dvr, precision=exact_prec
    )
    moment = inv_moment[None, :, None, None, None]
    rotation_term = (
        moment * (rot_level[None, None, None, None, :] + helicity[:, None, None, None, None]) * wave
    )
    padding = jnp.zeros((1,) + wave.shape[1:], jnp.float32)
    couple = coriolis[:, None, None, None, None]
    above = jnp.concatenate([wave[1:] * couple, padding], axis=0)
    below = jnp.concatenate([padding, wave[:-1] * couple], axis=0)
    coriolis_term = moment * ladder[None, None, None, None, :] * (above + below)
    return radial_term + bond_term + third_term + potential_term + rotation_term + coriolis_term


def local(
    wave_now,
    wave_prev,
    potential,
    angular_dvr,
    kinetic_radial,
    kinetic_bond,
    kinetic_third,
    inv_moment,
    rot_level,
    helicity,
    coriolis,
    ladder,
    damping,
    strip_bond,
    strip_third,
    strip_weight,
    strip_length,
    strip_owner,
    strip_cell,
):
    blocks, local_rows, bond_pts, thirds, angles = wave_now.shape
    flat_wave = wave_now.reshape(blocks, local_rows, bond_pts * thirds, angles)
    mixed = jnp.einsum(
        "ij,kjca->kica",
        kinetic_radial,
        lax.all_to_all(flat_wave, "slab", split_axis=2, concat_axis=1, tiled=True),
        precision=exact_prec,
    )
    radial_term = lax.all_to_all(mixed, "slab", split_axis=1, concat_axis=2, tiled=True).reshape(
        wave_now.shape
    )
    devices = lax.axis_size("slab")
    slot_count = max(2, 2 * SMAX // devices)
    points = local_rows * SMAX
    cells = wave_now.reshape(blocks, local_rows * bond_pts * thirds, angles)
    stencil_step = jnp.arange(4, dtype=jnp.int32)
    offset = jnp.arange(local_rows, dtype=jnp.int32)[:, None, None] * (bond_pts * thirds)
    cell_idx = (
        offset
        + (strip_bond[:, :, None] + stencil_step[None, None, :]) * thirds
        + strip_third[:, :, None]
    )
    stencil = jnp.take(cells, cell_idx.reshape(-1), axis=1).reshape(blocks, points, 4, angles)
    weights = strip_weight.reshape(points, 4)
    surface = jnp.einsum("pt,kpta->kpa", weights, stencil, precision=exact_prec)
    alive_mask = (
        (jnp.arange(SMAX, dtype=jnp.int32)[None, :] < strip_length[:, None])
        .reshape(points)
        .astype(jnp.float32)
    )
    surface = surface * alive_mask[None, :, None]
    owner = strip_owner.reshape(points)
    onehot = (owner[:, None] == jnp.arange(devices, dtype=jnp.int32)[None, :]).astype(jnp.float32)
    point_iota = jnp.arange(points, dtype=jnp.int32)
    earlier = (point_iota[None, :] < point_iota[:, None]).astype(jnp.float32)
    before = jnp.dot(earlier, onehot, precision=exact_prec)
    order_in = jnp.sum(onehot * before, axis=1).astype(jnp.int32)
    slot_idx = owner * slot_count + order_in
    select = (
        slot_idx[None, :] == jnp.arange(devices * slot_count, dtype=jnp.int32)[:, None]
    ).astype(jnp.float32)
    values = jnp.einsum("qp,kpa->qka", select, surface, precision=exact_prec).reshape(
        devices, slot_count, blocks, angles
    )
    cell_ids = jnp.dot(
        select, strip_cell.reshape(points).astype(jnp.float32), precision=exact_prec
    ).reshape(devices, slot_count)
    got_values, got_cells = (
        lax.all_to_all(values, "slab", split_axis=0, concat_axis=0, tiled=True),
        lax.all_to_all(cell_ids, "slab", split_axis=0, concat_axis=0, tiled=True),
    )
    landing = (
        got_cells.reshape(-1)[None, :] == jnp.arange(P_DEV, dtype=jnp.float32)[:, None]
    ).astype(jnp.float32)
    surface_flux = jnp.einsum(
        "cq,qka->kca",
        landing,
        got_values.reshape(devices * slot_count, blocks, angles),
        precision=exact_prec,
    )
    hamiltonian = hamiltonian_apply(
        wave_now,
        radial_term,
        potential,
        angular_dvr,
        kinetic_bond,
        kinetic_third,
        inv_moment,
        rot_level,
        helicity,
        coriolis,
        ladder,
    )
    damp = damping[None, :, :, :, None]
    wave_next = damp * (0.5 * hamiltonian - damp * wave_prev)
    return (wave_next, surface_flux)


def split_dot(onehot, values):
    high = lax.reduce_precision(values, exponent_bits=8, mantissa_bits=7)
    both = jnp.concatenate([high, values - high], axis=-1).astype(jnp.bfloat16)
    out = jnp.dot(onehot, both, preferred_element_type=jnp.float32)
    width = values.shape[-1]
    return out[:, :width] + out[:, width:]


def local_blocks(
    wave_now,
    wave_prev,
    potential,
    angular_dvr,
    kinetic_radial,
    kinetic_bond,
    kinetic_third,
    inv_moment,
    rot_level,
    helicity,
    coriolis,
    ladder,
    damping,
    strip_bond,
    strip_third,
    strip_weight,
    strip_length,
    strip_owner,
    strip_cell,
):
    blocks, _, bond_pts, thirds, angles = wave_now.shape
    devices = lax.axis_size("slab")
    cells = bond_pts * thirds
    points = strip_bond.shape[1]
    cuts = devices // blocks
    width = angles // cuts
    high_prec = lax.Precision.HIGH
    wave = wave_now.reshape(blocks, cells, angles)

    live = jnp.arange(points, dtype=jnp.int32)[None, :] < strip_length[:, None]
    weights = jnp.where(live[:, :, None], strip_weight, 0.0)[0].T
    base = (strip_bond * thirds + strip_third).astype(jnp.float32)
    target = (strip_owner[:, :, 0] * P_DEV + strip_cell).astype(jnp.float32)
    table = jnp.concatenate([base, target, weights, jnp.zeros((2, points), jnp.float32)], axis=0)
    packed = wave.reshape(blocks, cells, cuts, width).transpose(0, 2, 1, 3)
    packed = packed.reshape(devices, cells, width)
    packed = jnp.concatenate(
        [packed, jnp.broadcast_to(table[None], (devices,) + table.shape)], axis=1
    )
    got = lax.all_to_all(packed, "slab", split_axis=0, concat_axis=0, tiled=True)
    field = got[:, :cells]
    info = got[:, cells:]

    mixed = jnp.einsum("ij,jca->ica", kinetic_radial, field, precision=high_prec)
    cell_iota = jnp.arange(cells, dtype=jnp.float32)[None, None, :]
    stencil = sum(
        jnp.where(cell_iota == info[:, 0, :, None] + float(t * thirds), info[:, 2 + t, :, None], 0.0)
        for t in range(4)
    )
    surface = jnp.einsum("qpc,qca->qpa", stencil, field, precision=high_prec)
    product_iota = jnp.arange(devices * P_DEV, dtype=jnp.float32)[:, None]
    landing = (product_iota == info[:, 1, :].reshape(-1)[None, :]).astype(jnp.bfloat16)
    flux = split_dot(landing, surface.reshape(devices * points, width))
    back = jnp.concatenate([mixed, flux.reshape(devices, P_DEV, width)], axis=1)
    back = lax.all_to_all(back, "slab", split_axis=0, concat_axis=0, tiled=True)
    back = back.reshape(blocks, cuts, cells + P_DEV, width)
    radial_term = back[:, :, :cells].transpose(0, 2, 1, 3).reshape(blocks, cells, angles)
    surface_flux = back[:, :, cells:].transpose(0, 2, 1, 3).reshape(blocks, P_DEV, angles)

    kinetic = (
        kinetic_bond[:, None, :, None] * jnp.eye(thirds, dtype=jnp.float32)[None, :, None, :]
        + jnp.eye(bond_pts, dtype=jnp.float32)[:, None, :, None] * kinetic_third[None, :, None, :]
    ).reshape(cells, cells)
    kinetic_term = jnp.einsum("cd,kda->kca", kinetic, wave, precision=high_prec)
    grid_wave = jnp.einsum("kcb,ba->kca", wave, angular_dvr, precision=high_prec)
    potential_term = jnp.einsum(
        "kca,ba->kcb",
        potential.reshape(1, cells, angles) * grid_wave,
        angular_dvr,
        precision=high_prec,
    )
    moment = inv_moment[0]
    rotation_term = moment * (rot_level[None, None, :] + helicity[:, None, None]) * wave
    padding = jnp.zeros((1,) + wave.shape[1:], jnp.float32)
    couple = coriolis[:, None, None]
    above = jnp.concatenate([wave[1:] * couple, padding], axis=0)
    below = jnp.concatenate([padding, wave[:-1] * couple], axis=0)
    coriolis_term = moment * ladder[None, None, :] * (above + below)
    damp = damping.reshape(1, cells, 1)
    own = kinetic_term + potential_term + rotation_term + coriolis_term
    wave_next = damp * (0.5 * (radial_term + own) - damp * wave_prev.reshape(wave.shape))
    return wave_next.reshape(wave_now.shape), surface_flux


def plan(*args):
    blocks, local_rows, _, _, angles = args[0].shape
    devices = lax.axis_size("slab")
    cuts = devices // blocks
    fits = (
        local_rows == 1
        and devices % blocks == 0
        and angles % max(cuts, 1) == 0
        and angles // max(cuts, 1) == args[13].shape[1]
    )
    return local_blocks(*args) if fits else local(*args)


def solution(mesh):
    in_specs = (
        P("groups", "slab", None, None, None),
        P("groups", "slab", None, None, None),
        P("slab", None, None, None),
        P(),
        P(),
        P(),
        P(),
        P("slab"),
        P(),
        P(),
        P(),
        P(),
        P("slab", None, None),
        P("slab", None),
        P("slab", None),
        P("slab", None, None),
        P("slab"),
        P("slab", None, None),
        P("slab", None),
    )
    out_specs = (P("groups", "slab", None, None, None), P("groups", "slab", None))
    return jax.shard_map(plan, mesh=mesh, in_specs=in_specs, out_specs=out_specs, check_vma=False)
```

```python
import jax
import jax.numpy as jnp
from jax import lax
from jax.experimental import pallas as pl
from jax.experimental.pallas import tpu as pltpu
from jax.sharding import PartitionSpec as P

SMAX = 128
P_DEV = 64


exact_prec = lax.Precision.HIGHEST


def hamiltonian_apply(
    wave,
    radial_term,
    potential,
    angular_dvr,
    kinetic_bond,
    kinetic_third,
    inv_moment,
    rot_level,
    helicity,
    coriolis,
    ladder,
):
    bond_term = jnp.einsum("ij,kqjza->kqiza", kinetic_bond, wave, precision=exact_prec)
    third_term = jnp.einsum("ij,kqrja->kqria", kinetic_third, wave, precision=exact_prec)
    grid_wave = jnp.einsum("kqrzb,ba->kqrza", wave, angular_dvr, precision=exact_prec)
    potential_term = jnp.einsum(
        "kqrza,ba->kqrzb", potential[None] * grid_wave, angular_dvr, precision=exact_prec
    )
    moment = inv_moment[None, :, None, None, None]
    rotation_term = (
        moment * (rot_level[None, None, None, None, :] + helicity[:, None, None, None, None]) * wave
    )
    padding = jnp.zeros((1,) + wave.shape[1:], jnp.float32)
    couple = coriolis[:, None, None, None, None]
    above = jnp.concatenate([wave[1:] * couple, padding], axis=0)
    below = jnp.concatenate([padding, wave[:-1] * couple], axis=0)
    coriolis_term = moment * ladder[None, None, None, None, :] * (above + below)
    return radial_term + bond_term + third_term + potential_term + rotation_term + coriolis_term


def local(
    wave_now,
    wave_prev,
    potential,
    angular_dvr,
    kinetic_radial,
    kinetic_bond,
    kinetic_third,
    inv_moment,
    rot_level,
    helicity,
    coriolis,
    ladder,
    damping,
    strip_bond,
    strip_third,
    strip_weight,
    strip_length,
    strip_owner,
    strip_cell,
):
    blocks, local_rows, bond_pts, thirds, angles = wave_now.shape
    flat_wave = wave_now.reshape(blocks, local_rows, bond_pts * thirds, angles)
    mixed = jnp.einsum(
        "ij,kjca->kica",
        kinetic_radial,
        lax.all_to_all(flat_wave, "slab", split_axis=2, concat_axis=1, tiled=True),
        precision=exact_prec,
    )
    radial_term = lax.all_to_all(mixed, "slab", split_axis=1, concat_axis=2, tiled=True).reshape(
        wave_now.shape
    )
    devices = lax.axis_size("slab")
    slot_count = max(2, 2 * SMAX // devices)
    points = local_rows * SMAX
    cells = wave_now.reshape(blocks, local_rows * bond_pts * thirds, angles)
    stencil_step = jnp.arange(4, dtype=jnp.int32)
    offset = jnp.arange(local_rows, dtype=jnp.int32)[:, None, None] * (bond_pts * thirds)
    cell_idx = (
        offset
        + (strip_bond[:, :, None] + stencil_step[None, None, :]) * thirds
        + strip_third[:, :, None]
    )
    stencil = jnp.take(cells, cell_idx.reshape(-1), axis=1).reshape(blocks, points, 4, angles)
    weights = strip_weight.reshape(points, 4)
    surface = jnp.einsum("pt,kpta->kpa", weights, stencil, precision=exact_prec)
    alive_mask = (
        (jnp.arange(SMAX, dtype=jnp.int32)[None, :] < strip_length[:, None])
        .reshape(points)
        .astype(jnp.float32)
    )
    surface = surface * alive_mask[None, :, None]
    owner = strip_owner.reshape(points)
    onehot = (owner[:, None] == jnp.arange(devices, dtype=jnp.int32)[None, :]).astype(jnp.float32)
    point_iota = jnp.arange(points, dtype=jnp.int32)
    earlier = (point_iota[None, :] < point_iota[:, None]).astype(jnp.float32)
    before = jnp.dot(earlier, onehot, precision=exact_prec)
    order_in = jnp.sum(onehot * before, axis=1).astype(jnp.int32)
    slot_idx = owner * slot_count + order_in
    select = (
        slot_idx[None, :] == jnp.arange(devices * slot_count, dtype=jnp.int32)[:, None]
    ).astype(jnp.float32)
    values = jnp.einsum("qp,kpa->qka", select, surface, precision=exact_prec).reshape(
        devices, slot_count, blocks, angles
    )
    cell_ids = jnp.dot(
        select, strip_cell.reshape(points).astype(jnp.float32), precision=exact_prec
    ).reshape(devices, slot_count)
    got_values, got_cells = (
        lax.all_to_all(values, "slab", split_axis=0, concat_axis=0, tiled=True),
        lax.all_to_all(cell_ids, "slab", split_axis=0, concat_axis=0, tiled=True),
    )
    landing = (
        got_cells.reshape(-1)[None, :] == jnp.arange(P_DEV, dtype=jnp.float32)[:, None]
    ).astype(jnp.float32)
    surface_flux = jnp.einsum(
        "cq,qka->kca",
        landing,
        got_values.reshape(devices * slot_count, blocks, angles),
        precision=exact_prec,
    )
    hamiltonian = hamiltonian_apply(
        wave_now,
        radial_term,
        potential,
        angular_dvr,
        kinetic_bond,
        kinetic_third,
        inv_moment,
        rot_level,
        helicity,
        coriolis,
        ladder,
    )
    damp = damping[None, :, :, :, None]
    wave_next = damp * (0.5 * hamiltonian - damp * wave_prev)
    return (wave_next, surface_flux)


def split_dot(onehot, values):
    high = lax.reduce_precision(values, exponent_bits=8, mantissa_bits=7)
    both = jnp.concatenate([high, values - high], axis=-1).astype(jnp.bfloat16)
    out = jnp.dot(onehot, both, preferred_element_type=jnp.float32)
    width = values.shape[-1]
    return out[:, :width] + out[:, width:]


def finish_kernel(back_ref, own_ref, prev_ref, damp_ref, next_ref, flux_ref):
    cells = own_ref.shape[1]
    cuts = back_ref.shape[0]
    width = back_ref.shape[2]
    damp = damp_ref[...]
    for cut in range(cuts):
        lanes = slice(cut * width, (cut + 1) * width)
        total = back_ref[cut, :cells, :] + own_ref[0, :, lanes]
        next_ref[0, :, lanes] = damp * (0.5 * total - damp * prev_ref[0, :, lanes])
        flux_ref[0, :, lanes] = back_ref[cut, cells:, :]


def finish(back, own, prev, damp):
    blocks, cells, angles = own.shape
    devices, rows, width = back.shape
    parts = 2
    cuts = devices // blocks // parts
    whole = pl.BlockSpec((1, cells, cuts * width), lambda k, h: (k, 0, h))
    return pl.pallas_call(
        finish_kernel,
        grid=(blocks, parts),
        in_specs=[
            pl.BlockSpec((cuts, rows, width), lambda k, h: (k * parts + h, 0, 0)),
            whole,
            whole,
            pl.BlockSpec((cells, 1), lambda k, h: (0, 0)),
        ],
        out_specs=[
            whole,
            pl.BlockSpec((1, rows - cells, cuts * width), lambda k, h: (k, 0, h)),
        ],
        out_shape=[
            jax.ShapeDtypeStruct((blocks, cells, angles), jnp.float32),
            jax.ShapeDtypeStruct((blocks, rows - cells, angles), jnp.float32),
        ],
    )(back, own, prev, damp)


def local_blocks(
    wave_now,
    wave_prev,
    potential,
    angular_dvr,
    kinetic_radial,
    kinetic_bond,
    kinetic_third,
    inv_moment,
    rot_level,
    helicity,
    coriolis,
    ladder,
    damping,
    strip_bond,
    strip_third,
    strip_weight,
    strip_length,
    strip_owner,
    strip_cell,
):
    blocks, _, bond_pts, thirds, angles = wave_now.shape
    devices = lax.axis_size("slab")
    cells = bond_pts * thirds
    points = strip_bond.shape[1]
    cuts = devices // blocks
    width = angles // cuts
    high_prec = lax.Precision.HIGH
    wave = wave_now.reshape(blocks, cells, angles)

    live = jnp.arange(points, dtype=jnp.int32)[None, :] < strip_length[:, None]
    weights = jnp.where(live[:, :, None], strip_weight, 0.0)[0].T
    base = (strip_bond * thirds + strip_third).astype(jnp.float32)
    target = (strip_owner[:, :, 0] * P_DEV + strip_cell).astype(jnp.float32)
    table = jnp.concatenate([base, target, weights, jnp.zeros((2, points), jnp.float32)], axis=0)
    packed = wave.reshape(blocks, cells, cuts, width).transpose(0, 2, 1, 3)
    packed = packed.reshape(devices, cells, width)
    packed = jnp.concatenate(
        [packed, jnp.broadcast_to(table[None], (devices,) + table.shape)], axis=1
    )
    got = lax.all_to_all(packed, "slab", split_axis=0, concat_axis=0, tiled=True)
    field = got[:, :cells]
    info = got[:, cells:]

    mixed = jnp.einsum("ij,jca->ica", kinetic_radial, field, precision=high_prec)
    cell_iota = jnp.arange(cells, dtype=jnp.float32)[None, None, :]
    stencil = sum(
        jnp.where(cell_iota == info[:, 0, :, None] + float(t * thirds), info[:, 2 + t, :, None], 0.0)
        for t in range(4)
    )
    surface = jnp.einsum("qpc,qca->qpa", stencil, field, precision=high_prec)
    product_iota = jnp.arange(devices * P_DEV, dtype=jnp.float32)[:, None]
    landing = (product_iota == info[:, 1, :].reshape(-1)[None, :]).astype(jnp.bfloat16)
    flux = split_dot(landing, surface.reshape(devices * points, width))
    back = jnp.concatenate([mixed, flux.reshape(devices, P_DEV, width)], axis=1)
    back = lax.all_to_all(back, "slab", split_axis=0, concat_axis=0, tiled=True)

    kinetic = (
        kinetic_bond[:, None, :, None] * jnp.eye(thirds, dtype=jnp.float32)[None, :, None, :]
        + jnp.eye(bond_pts, dtype=jnp.float32)[:, None, :, None] * kinetic_third[None, :, None, :]
    ).reshape(cells, cells)
    kinetic_term = jnp.einsum("cd,kda->kca", kinetic, wave, precision=high_prec)
    grid_wave = jnp.einsum("kcb,ba->kca", wave, angular_dvr, precision=high_prec)
    potential_term = jnp.einsum(
        "kca,ba->kcb",
        potential.reshape(1, cells, angles) * grid_wave,
        angular_dvr,
        precision=high_prec,
    )
    moment = inv_moment[0]
    rotation_term = moment * (rot_level[None, None, :] + helicity[:, None, None]) * wave
    padding = jnp.zeros((1,) + wave.shape[1:], jnp.float32)
    couple = coriolis[:, None, None]
    above = jnp.concatenate([wave[1:] * couple, padding], axis=0)
    below = jnp.concatenate([padding, wave[:-1] * couple], axis=0)
    coriolis_term = moment * ladder[None, None, :] * (above + below)
    own = kinetic_term + potential_term + rotation_term + coriolis_term
    wave_next, surface_flux = finish(
        back, own, wave_prev.reshape(wave.shape), damping.reshape(cells, 1)
    )
    return wave_next.reshape(wave_now.shape), surface_flux


def plan(*args):
    blocks, local_rows, _, _, angles = args[0].shape
    devices = lax.axis_size("slab")
    cuts = devices // blocks
    fits = (
        local_rows == 1
        and devices % blocks == 0
        and angles % max(cuts, 1) == 0
        and angles // max(cuts, 1) == args[13].shape[1]
        and cuts % 2 == 0
    )
    return local_blocks(*args) if fits else local(*args)


def solution(mesh):
    in_specs = (
        P("groups", "slab", None, None, None),
        P("groups", "slab", None, None, None),
        P("slab", None, None, None),
        P(),
        P(),
        P(),
        P(),
        P("slab"),
        P(),
        P(),
        P(),
        P(),
        P("slab", None, None),
        P("slab", None),
        P("slab", None),
        P("slab", None, None),
        P("slab"),
        P("slab", None, None),
        P("slab", None),
    )
    out_specs = (P("groups", "slab", None, None, None), P("groups", "slab", None))
    return jax.shard_map(plan, mesh=mesh, in_specs=in_specs, out_specs=out_specs, check_vma=False)
```

```python
import functools

import jax
import jax.numpy as jnp
from jax import lax
from jax.experimental import pallas as pl
from jax.experimental.pallas import tpu as pltpu
from jax.sharding import PartitionSpec as P

SMAX = 128
P_DEV = 64


exact_prec = lax.Precision.HIGHEST


def hamiltonian_apply(
    wave,
    radial_term,
    potential,
    angular_dvr,
    kinetic_bond,
    kinetic_third,
    inv_moment,
    rot_level,
    helicity,
    coriolis,
    ladder,
):
    bond_term = jnp.einsum("ij,kqjza->kqiza", kinetic_bond, wave, precision=exact_prec)
    third_term = jnp.einsum("ij,kqrja->kqria", kinetic_third, wave, precision=exact_prec)
    grid_wave = jnp.einsum("kqrzb,ba->kqrza", wave, angular_dvr, precision=exact_prec)
    potential_term = jnp.einsum(
        "kqrza,ba->kqrzb", potential[None] * grid_wave, angular_dvr, precision=exact_prec
    )
    moment = inv_moment[None, :, None, None, None]
    rotation_term = (
        moment * (rot_level[None, None, None, None, :] + helicity[:, None, None, None, None]) * wave
    )
    padding = jnp.zeros((1,) + wave.shape[1:], jnp.float32)
    couple = coriolis[:, None, None, None, None]
    above = jnp.concatenate([wave[1:] * couple, padding], axis=0)
    below = jnp.concatenate([padding, wave[:-1] * couple], axis=0)
    coriolis_term = moment * ladder[None, None, None, None, :] * (above + below)
    return radial_term + bond_term + third_term + potential_term + rotation_term + coriolis_term


def local(
    wave_now,
    wave_prev,
    potential,
    angular_dvr,
    kinetic_radial,
    kinetic_bond,
    kinetic_third,
    inv_moment,
    rot_level,
    helicity,
    coriolis,
    ladder,
    damping,
    strip_bond,
    strip_third,
    strip_weight,
    strip_length,
    strip_owner,
    strip_cell,
):
    blocks, local_rows, bond_pts, thirds, angles = wave_now.shape
    flat_wave = wave_now.reshape(blocks, local_rows, bond_pts * thirds, angles)
    mixed = jnp.einsum(
        "ij,kjca->kica",
        kinetic_radial,
        lax.all_to_all(flat_wave, "slab", split_axis=2, concat_axis=1, tiled=True),
        precision=exact_prec,
    )
    radial_term = lax.all_to_all(mixed, "slab", split_axis=1, concat_axis=2, tiled=True).reshape(
        wave_now.shape
    )
    devices = lax.axis_size("slab")
    slot_count = max(2, 2 * SMAX // devices)
    points = local_rows * SMAX
    cells = wave_now.reshape(blocks, local_rows * bond_pts * thirds, angles)
    stencil_step = jnp.arange(4, dtype=jnp.int32)
    offset = jnp.arange(local_rows, dtype=jnp.int32)[:, None, None] * (bond_pts * thirds)
    cell_idx = (
        offset
        + (strip_bond[:, :, None] + stencil_step[None, None, :]) * thirds
        + strip_third[:, :, None]
    )
    stencil = jnp.take(cells, cell_idx.reshape(-1), axis=1).reshape(blocks, points, 4, angles)
    weights = strip_weight.reshape(points, 4)
    surface = jnp.einsum("pt,kpta->kpa", weights, stencil, precision=exact_prec)
    alive_mask = (
        (jnp.arange(SMAX, dtype=jnp.int32)[None, :] < strip_length[:, None])
        .reshape(points)
        .astype(jnp.float32)
    )
    surface = surface * alive_mask[None, :, None]
    owner = strip_owner.reshape(points)
    onehot = (owner[:, None] == jnp.arange(devices, dtype=jnp.int32)[None, :]).astype(jnp.float32)
    point_iota = jnp.arange(points, dtype=jnp.int32)
    earlier = (point_iota[None, :] < point_iota[:, None]).astype(jnp.float32)
    before = jnp.dot(earlier, onehot, precision=exact_prec)
    order_in = jnp.sum(onehot * before, axis=1).astype(jnp.int32)
    slot_idx = owner * slot_count + order_in
    select = (
        slot_idx[None, :] == jnp.arange(devices * slot_count, dtype=jnp.int32)[:, None]
    ).astype(jnp.float32)
    values = jnp.einsum("qp,kpa->qka", select, surface, precision=exact_prec).reshape(
        devices, slot_count, blocks, angles
    )
    cell_ids = jnp.dot(
        select, strip_cell.reshape(points).astype(jnp.float32), precision=exact_prec
    ).reshape(devices, slot_count)
    got_values, got_cells = (
        lax.all_to_all(values, "slab", split_axis=0, concat_axis=0, tiled=True),
        lax.all_to_all(cell_ids, "slab", split_axis=0, concat_axis=0, tiled=True),
    )
    landing = (
        got_cells.reshape(-1)[None, :] == jnp.arange(P_DEV, dtype=jnp.float32)[:, None]
    ).astype(jnp.float32)
    surface_flux = jnp.einsum(
        "cq,qka->kca",
        landing,
        got_values.reshape(devices * slot_count, blocks, angles),
        precision=exact_prec,
    )
    hamiltonian = hamiltonian_apply(
        wave_now,
        radial_term,
        potential,
        angular_dvr,
        kinetic_bond,
        kinetic_third,
        inv_moment,
        rot_level,
        helicity,
        coriolis,
        ladder,
    )
    damp = damping[None, :, :, :, None]
    wave_next = damp * (0.5 * hamiltonian - damp * wave_prev)
    return (wave_next, surface_flux)


def split_dot(onehot, values):
    high = lax.reduce_precision(values, exponent_bits=8, mantissa_bits=7)
    both = jnp.concatenate([high, values - high], axis=-1).astype(jnp.bfloat16)
    out = jnp.dot(onehot, both, preferred_element_type=jnp.float32)
    width = values.shape[-1]
    return out[:, :width] + out[:, width:]


def finish_kernel(back_ref, own_ref, prev_ref, damp_ref, next_ref, flux_ref):
    cells = own_ref.shape[1]
    cuts = back_ref.shape[0]
    width = back_ref.shape[2]
    damp = damp_ref[...]
    for cut in range(cuts):
        lanes = slice(cut * width, (cut + 1) * width)
        total = back_ref[cut, :cells, :] + own_ref[0, :, lanes]
        next_ref[0, :, lanes] = damp * (0.5 * total - damp * prev_ref[0, :, lanes])
        flux_ref[0, :, lanes] = back_ref[cut, cells:, :]


def finish(back, own, prev, damp):
    blocks, cells, angles = own.shape
    devices, rows, width = back.shape
    parts = 2
    cuts = devices // blocks // parts
    whole = pl.BlockSpec((1, cells, cuts * width), lambda k, h: (k, 0, h))
    return pl.pallas_call(
        finish_kernel,
        grid=(blocks, parts),
        in_specs=[
            pl.BlockSpec((cuts, rows, width), lambda k, h: (k * parts + h, 0, 0)),
            whole,
            whole,
            pl.BlockSpec((cells, 1), lambda k, h: (0, 0)),
        ],
        out_specs=[
            whole,
            pl.BlockSpec((1, rows - cells, cuts * width), lambda k, h: (k, 0, h)),
        ],
        out_shape=[
            jax.ShapeDtypeStruct((blocks, cells, angles), jnp.float32),
            jax.ShapeDtypeStruct((blocks, rows - cells, angles), jnp.float32),
        ],
    )(back, own, prev, damp)


def spread_kernel(devices, wave_ref, table_ref, field_ref, info_ref, send_sem, recv_sem, own_sem):
    blocks, _, angles = wave_ref.shape
    cuts = devices // blocks
    width = angles // cuts
    me = lax.axis_index("slab")
    barrier = pltpu.get_barrier_semaphore()
    for step in range(1, devices):
        pl.semaphore_signal(
            barrier,
            inc=1,
            device_id={"slab": lax.rem(me + step, devices)},
            device_id_type=pl.DeviceIdType.MESH,
        )

    def block(peer):
        lane = pl.multiple_of(lax.rem(peer, cuts) * width, width)
        return wave_ref.at[peer // cuts, :, pl.ds(lane, width)]

    own = [
        pltpu.make_async_copy(block(me), field_ref.at[me], own_sem.at[0]),
        pltpu.make_async_copy(table_ref, info_ref.at[me], own_sem.at[1]),
    ]
    for copy in own:
        copy.start()
    pl.semaphore_wait(barrier, devices - 1)

    steps = sorted(range(1, devices), key=lambda step: abs(step - devices // 2))
    copies = []
    for step in steps:
        peer = lax.rem(me + step, devices)
        pairs = ((block(peer), field_ref.at[me]), (table_ref, info_ref.at[me]))
        for part, (source, target) in enumerate(pairs):
            copy = pltpu.make_async_remote_copy(
                src_ref=source,
                dst_ref=target,
                send_sem=send_sem.at[part, step],
                recv_sem=recv_sem.at[part, step],
                device_id={"slab": peer},
                device_id_type=pl.DeviceIdType.MESH,
            )
            copy.start()
            copies.append(copy)
    for copy in own:
        copy.wait()
    for step in steps:
        sender = lax.rem(me + devices - step, devices)
        pairs = ((block(me), field_ref.at[sender]), (table_ref, info_ref.at[sender]))
        for part, (source, target) in enumerate(pairs):
            pltpu.make_async_remote_copy(
                src_ref=source,
                dst_ref=target,
                send_sem=send_sem.at[part, step],
                recv_sem=recv_sem.at[part, step],
                device_id={"slab": sender},
                device_id_type=pl.DeviceIdType.MESH,
            ).wait_recv()
    for copy in copies:
        copy.wait_send()


def spread(wave, table):
    blocks, cells, angles = wave.shape
    devices = lax.axis_size("slab")
    width = angles // (devices // blocks)
    return pl.pallas_call(
        functools.partial(spread_kernel, devices),
        in_specs=[pl.BlockSpec(memory_space=pl.ANY)] * 2,
        out_specs=[pl.BlockSpec(memory_space=pl.ANY)] * 2,
        out_shape=[
            jax.ShapeDtypeStruct((devices, cells, width), jnp.float32),
            jax.ShapeDtypeStruct((devices,) + table.shape, jnp.float32),
        ],
        scratch_shapes=[
            pltpu.SemaphoreType.DMA((2, devices)),
            pltpu.SemaphoreType.DMA((2, devices)),
            pltpu.SemaphoreType.DMA((2,)),
        ],
        compiler_params=pltpu.CompilerParams(collective_id=0, has_side_effects=True),
    )(wave, table)


def local_blocks(
    wave_now,
    wave_prev,
    potential,
    angular_dvr,
    kinetic_radial,
    kinetic_bond,
    kinetic_third,
    inv_moment,
    rot_level,
    helicity,
    coriolis,
    ladder,
    damping,
    strip_bond,
    strip_third,
    strip_weight,
    strip_length,
    strip_owner,
    strip_cell,
):
    blocks, _, bond_pts, thirds, angles = wave_now.shape
    devices = lax.axis_size("slab")
    cells = bond_pts * thirds
    points = strip_bond.shape[1]
    cuts = devices // blocks
    width = angles // cuts
    high_prec = lax.Precision.HIGH
    wave = wave_now.reshape(blocks, cells, angles)

    live = jnp.arange(points, dtype=jnp.int32)[None, :] < strip_length[:, None]
    weights = jnp.where(live[:, :, None], strip_weight, 0.0)[0].T
    base = (strip_bond * thirds + strip_third).astype(jnp.float32)
    target = (strip_owner[:, :, 0] * P_DEV + strip_cell).astype(jnp.float32)
    table = jnp.concatenate([base, target, weights, jnp.zeros((2, points), jnp.float32)], axis=0)
    field, info = spread(wave, table)

    mixed = jnp.einsum("ij,jca->ica", kinetic_radial, field, precision=high_prec)
    cell_iota = jnp.arange(cells, dtype=jnp.float32)[None, None, :]
    stencil = sum(
        jnp.where(cell_iota == info[:, 0, :, None] + float(t * thirds), info[:, 2 + t, :, None], 0.0)
        for t in range(4)
    )
    surface = jnp.einsum("qpc,qca->qpa", stencil, field, precision=high_prec)
    product_iota = jnp.arange(devices * P_DEV, dtype=jnp.float32)[:, None]
    landing = (product_iota == info[:, 1, :].reshape(-1)[None, :]).astype(jnp.bfloat16)
    flux = split_dot(landing, surface.reshape(devices * points, width))
    back = jnp.concatenate([mixed, flux.reshape(devices, P_DEV, width)], axis=1)
    back = lax.all_to_all(back, "slab", split_axis=0, concat_axis=0, tiled=True)

    kinetic = (
        kinetic_bond[:, None, :, None] * jnp.eye(thirds, dtype=jnp.float32)[None, :, None, :]
        + jnp.eye(bond_pts, dtype=jnp.float32)[:, None, :, None] * kinetic_third[None, :, None, :]
    ).reshape(cells, cells)
    kinetic_term = jnp.einsum("cd,kda->kca", kinetic, wave, precision=high_prec)
    grid_wave = jnp.einsum("kcb,ba->kca", wave, angular_dvr, precision=high_prec)
    potential_term = jnp.einsum(
        "kca,ba->kcb",
        potential.reshape(1, cells, angles) * grid_wave,
        angular_dvr,
        precision=high_prec,
    )
    moment = inv_moment[0]
    rotation_term = moment * (rot_level[None, None, :] + helicity[:, None, None]) * wave
    padding = jnp.zeros((1,) + wave.shape[1:], jnp.float32)
    couple = coriolis[:, None, None]
    above = jnp.concatenate([wave[1:] * couple, padding], axis=0)
    below = jnp.concatenate([padding, wave[:-1] * couple], axis=0)
    coriolis_term = moment * ladder[None, None, :] * (above + below)
    own = kinetic_term + potential_term + rotation_term + coriolis_term
    wave_next, surface_flux = finish(
        back, own, wave_prev.reshape(wave.shape), damping.reshape(cells, 1)
    )
    return wave_next.reshape(wave_now.shape), surface_flux


def plan(*args):
    blocks, local_rows, _, _, angles = args[0].shape
    devices = lax.axis_size("slab")
    cuts = devices // blocks
    fits = (
        local_rows == 1
        and devices % blocks == 0
        and angles % max(cuts, 1) == 0
        and angles // max(cuts, 1) == args[13].shape[1]
        and cuts % 2 == 0
    )
    return local_blocks(*args) if fits else local(*args)


def solution(mesh):
    in_specs = (
        P("groups", "slab", None, None, None),
        P("groups", "slab", None, None, None),
        P("slab", None, None, None),
        P(),
        P(),
        P(),
        P(),
        P("slab"),
        P(),
        P(),
        P(),
        P(),
        P("slab", None, None),
        P("slab", None),
        P("slab", None),
        P("slab", None, None),
        P("slab"),
        P("slab", None, None),
        P("slab", None),
    )
    out_specs = (P("groups", "slab", None, None, None), P("groups", "slab", None))
    return jax.shard_map(plan, mesh=mesh, in_specs=in_specs, out_specs=out_specs, check_vma=False)
```

```python
import functools

import jax
import jax.numpy as jnp
from jax import lax
from jax.experimental import pallas as pl
from jax.experimental.pallas import tpu as pltpu
from jax.sharding import PartitionSpec as P

SMAX = 128
P_DEV = 64


exact_prec = lax.Precision.HIGHEST


def hamiltonian_apply(
    wave,
    radial_term,
    potential,
    angular_dvr,
    kinetic_bond,
    kinetic_third,
    inv_moment,
    rot_level,
    helicity,
    coriolis,
    ladder,
):
    bond_term = jnp.einsum("ij,kqjza->kqiza", kinetic_bond, wave, precision=exact_prec)
    third_term = jnp.einsum("ij,kqrja->kqria", kinetic_third, wave, precision=exact_prec)
    grid_wave = jnp.einsum("kqrzb,ba->kqrza", wave, angular_dvr, precision=exact_prec)
    potential_term = jnp.einsum(
        "kqrza,ba->kqrzb", potential[None] * grid_wave, angular_dvr, precision=exact_prec
    )
    moment = inv_moment[None, :, None, None, None]
    rotation_term = (
        moment * (rot_level[None, None, None, None, :] + helicity[:, None, None, None, None]) * wave
    )
    padding = jnp.zeros((1,) + wave.shape[1:], jnp.float32)
    couple = coriolis[:, None, None, None, None]
    above = jnp.concatenate([wave[1:] * couple, padding], axis=0)
    below = jnp.concatenate([padding, wave[:-1] * couple], axis=0)
    coriolis_term = moment * ladder[None, None, None, None, :] * (above + below)
    return radial_term + bond_term + third_term + potential_term + rotation_term + coriolis_term


def local(
    wave_now,
    wave_prev,
    potential,
    angular_dvr,
    kinetic_radial,
    kinetic_bond,
    kinetic_third,
    inv_moment,
    rot_level,
    helicity,
    coriolis,
    ladder,
    damping,
    strip_bond,
    strip_third,
    strip_weight,
    strip_length,
    strip_owner,
    strip_cell,
):
    blocks, local_rows, bond_pts, thirds, angles = wave_now.shape
    flat_wave = wave_now.reshape(blocks, local_rows, bond_pts * thirds, angles)
    mixed = jnp.einsum(
        "ij,kjca->kica",
        kinetic_radial,
        lax.all_to_all(flat_wave, "slab", split_axis=2, concat_axis=1, tiled=True),
        precision=exact_prec,
    )
    radial_term = lax.all_to_all(mixed, "slab", split_axis=1, concat_axis=2, tiled=True).reshape(
        wave_now.shape
    )
    devices = lax.axis_size("slab")
    slot_count = max(2, 2 * SMAX // devices)
    points = local_rows * SMAX
    cells = wave_now.reshape(blocks, local_rows * bond_pts * thirds, angles)
    stencil_step = jnp.arange(4, dtype=jnp.int32)
    offset = jnp.arange(local_rows, dtype=jnp.int32)[:, None, None] * (bond_pts * thirds)
    cell_idx = (
        offset
        + (strip_bond[:, :, None] + stencil_step[None, None, :]) * thirds
        + strip_third[:, :, None]
    )
    stencil = jnp.take(cells, cell_idx.reshape(-1), axis=1).reshape(blocks, points, 4, angles)
    weights = strip_weight.reshape(points, 4)
    surface = jnp.einsum("pt,kpta->kpa", weights, stencil, precision=exact_prec)
    alive_mask = (
        (jnp.arange(SMAX, dtype=jnp.int32)[None, :] < strip_length[:, None])
        .reshape(points)
        .astype(jnp.float32)
    )
    surface = surface * alive_mask[None, :, None]
    owner = strip_owner.reshape(points)
    onehot = (owner[:, None] == jnp.arange(devices, dtype=jnp.int32)[None, :]).astype(jnp.float32)
    point_iota = jnp.arange(points, dtype=jnp.int32)
    earlier = (point_iota[None, :] < point_iota[:, None]).astype(jnp.float32)
    before = jnp.dot(earlier, onehot, precision=exact_prec)
    order_in = jnp.sum(onehot * before, axis=1).astype(jnp.int32)
    slot_idx = owner * slot_count + order_in
    select = (
        slot_idx[None, :] == jnp.arange(devices * slot_count, dtype=jnp.int32)[:, None]
    ).astype(jnp.float32)
    values = jnp.einsum("qp,kpa->qka", select, surface, precision=exact_prec).reshape(
        devices, slot_count, blocks, angles
    )
    cell_ids = jnp.dot(
        select, strip_cell.reshape(points).astype(jnp.float32), precision=exact_prec
    ).reshape(devices, slot_count)
    got_values, got_cells = (
        lax.all_to_all(values, "slab", split_axis=0, concat_axis=0, tiled=True),
        lax.all_to_all(cell_ids, "slab", split_axis=0, concat_axis=0, tiled=True),
    )
    landing = (
        got_cells.reshape(-1)[None, :] == jnp.arange(P_DEV, dtype=jnp.float32)[:, None]
    ).astype(jnp.float32)
    surface_flux = jnp.einsum(
        "cq,qka->kca",
        landing,
        got_values.reshape(devices * slot_count, blocks, angles),
        precision=exact_prec,
    )
    hamiltonian = hamiltonian_apply(
        wave_now,
        radial_term,
        potential,
        angular_dvr,
        kinetic_bond,
        kinetic_third,
        inv_moment,
        rot_level,
        helicity,
        coriolis,
        ladder,
    )
    damp = damping[None, :, :, :, None]
    wave_next = damp * (0.5 * hamiltonian - damp * wave_prev)
    return (wave_next, surface_flux)


def split_dot(onehot, values):
    high = lax.reduce_precision(values, exponent_bits=8, mantissa_bits=7)
    both = jnp.concatenate([high, values - high], axis=-1).astype(jnp.bfloat16)
    out = jnp.dot(onehot, both, preferred_element_type=jnp.float32)
    width = values.shape[-1]
    return out[:, :width] + out[:, width:]


def finish_kernel(back_ref, part_ref, own_ref, prev_ref, damp_ref, next_ref, flux_ref):
    cells = own_ref.shape[1]
    cuts = back_ref.shape[0]
    width = back_ref.shape[2]
    damp = damp_ref[...]
    for cut in range(cuts):
        lanes = slice(cut * width, (cut + 1) * width)
        total = back_ref[cut] + own_ref[0, :, lanes]
        next_ref[0, :, lanes] = damp * (0.5 * total - damp * prev_ref[0, :, lanes])
        flux_ref[0, :, lanes] = part_ref[cut]


def finish(back, flux, own, prev, damp):
    blocks, cells, angles = own.shape
    devices, _, width = back.shape
    rows = flux.shape[1]
    parts = 2
    cuts = devices // blocks // parts
    whole = pl.BlockSpec((1, cells, cuts * width), lambda k, h: (k, 0, h))
    return pl.pallas_call(
        finish_kernel,
        grid=(blocks, parts),
        in_specs=[
            pl.BlockSpec((cuts, cells, width), lambda k, h: (k * parts + h, 0, 0)),
            pl.BlockSpec((cuts, rows, width), lambda k, h: (k * parts + h, 0, 0)),
            whole,
            whole,
            pl.BlockSpec((cells, 1), lambda k, h: (0, 0)),
        ],
        out_specs=[
            whole,
            pl.BlockSpec((1, rows, cuts * width), lambda k, h: (k, 0, h)),
        ],
        out_shape=[
            jax.ShapeDtypeStruct((blocks, cells, angles), jnp.float32),
            jax.ShapeDtypeStruct((blocks, rows, angles), jnp.float32),
        ],
    )(back, flux, own, prev, damp)


def spread_kernel(devices, wave_ref, table_ref, field_ref, info_ref, send_sem, recv_sem, own_sem):
    blocks, _, angles = wave_ref.shape
    cuts = devices // blocks
    width = angles // cuts
    me = lax.axis_index("slab")
    barrier = pltpu.get_barrier_semaphore()
    for step in range(1, devices):
        pl.semaphore_signal(
            barrier,
            inc=1,
            device_id={"slab": lax.rem(me + step, devices)},
            device_id_type=pl.DeviceIdType.MESH,
        )

    def block(peer):
        lane = pl.multiple_of(lax.rem(peer, cuts) * width, width)
        return wave_ref.at[peer // cuts, :, pl.ds(lane, width)]

    own = [
        pltpu.make_async_copy(block(me), field_ref.at[me], own_sem.at[0]),
        pltpu.make_async_copy(table_ref, info_ref.at[me], own_sem.at[1]),
    ]
    for copy in own:
        copy.start()
    pl.semaphore_wait(barrier, devices - 1)

    steps = sorted(range(1, devices), key=lambda step: abs(step - devices // 2))
    copies = []
    for step in steps:
        peer = lax.rem(me + step, devices)
        pairs = ((block(peer), field_ref.at[me]), (table_ref, info_ref.at[me]))
        for part, (source, target) in enumerate(pairs):
            copy = pltpu.make_async_remote_copy(
                src_ref=source,
                dst_ref=target,
                send_sem=send_sem.at[part, step],
                recv_sem=recv_sem.at[part, step],
                device_id={"slab": peer},
                device_id_type=pl.DeviceIdType.MESH,
            )
            copy.start()
            copies.append(copy)
    for copy in own:
        copy.wait()
    for step in steps:
        sender = lax.rem(me + devices - step, devices)
        pairs = ((block(me), field_ref.at[sender]), (table_ref, info_ref.at[sender]))
        for part, (source, target) in enumerate(pairs):
            pltpu.make_async_remote_copy(
                src_ref=source,
                dst_ref=target,
                send_sem=send_sem.at[part, step],
                recv_sem=recv_sem.at[part, step],
                device_id={"slab": sender},
                device_id_type=pl.DeviceIdType.MESH,
            ).wait_recv()
    for copy in copies:
        copy.wait_send()


def spread(wave, table):
    blocks, cells, angles = wave.shape
    devices = lax.axis_size("slab")
    width = angles // (devices // blocks)
    return pl.pallas_call(
        functools.partial(spread_kernel, devices),
        in_specs=[pl.BlockSpec(memory_space=pl.ANY)] * 2,
        out_specs=[pl.BlockSpec(memory_space=pl.ANY)] * 2,
        out_shape=[
            jax.ShapeDtypeStruct((devices, cells, width), jnp.float32),
            jax.ShapeDtypeStruct((devices,) + table.shape, jnp.float32),
        ],
        scratch_shapes=[
            pltpu.SemaphoreType.DMA((2, devices)),
            pltpu.SemaphoreType.DMA((2, devices)),
            pltpu.SemaphoreType.DMA((2,)),
        ],
        compiler_params=pltpu.CompilerParams(collective_id=0, has_side_effects=True),
    )(wave, table)


def return_kernel(devices, flux_ref, out_ref, send_sem, recv_sem, own_sem):
    me = lax.axis_index("slab")
    barrier = pltpu.get_barrier_semaphore()
    for step in range(1, devices):
        pl.semaphore_signal(
            barrier,
            inc=1,
            device_id={"slab": lax.rem(me + step, devices)},
            device_id_type=pl.DeviceIdType.MESH,
        )

    def block(peer):
        return flux_ref.at[peer]

    own = [
        pltpu.make_async_copy(block(me), out_ref.at[me], own_sem.at[0]),
    ]
    for copy in own:
        copy.start()
    pl.semaphore_wait(barrier, devices - 1)

    steps = sorted(range(1, devices), key=lambda step: abs(step - devices // 2))
    copies = []
    for step in steps:
        peer = lax.rem(me + step, devices)
        pairs = ((block(peer), out_ref.at[me]),)
        for part, (source, target) in enumerate(pairs):
            copy = pltpu.make_async_remote_copy(
                src_ref=source,
                dst_ref=target,
                send_sem=send_sem.at[part, step],
                recv_sem=recv_sem.at[part, step],
                device_id={"slab": peer},
                device_id_type=pl.DeviceIdType.MESH,
            )
            copy.start()
            copies.append(copy)
    for copy in own:
        copy.wait()
    for step in steps:
        sender = lax.rem(me + devices - step, devices)
        pairs = ((block(me), out_ref.at[sender]),)
        for part, (source, target) in enumerate(pairs):
            pltpu.make_async_remote_copy(
                src_ref=source,
                dst_ref=target,
                send_sem=send_sem.at[part, step],
                recv_sem=recv_sem.at[part, step],
                device_id={"slab": sender},
                device_id_type=pl.DeviceIdType.MESH,
            ).wait_recv()
    for copy in copies:
        copy.wait_send()


def send_back(flux):
    devices = flux.shape[0]
    return pl.pallas_call(
        functools.partial(return_kernel, devices),
        in_specs=[pl.BlockSpec(memory_space=pl.ANY)],
        out_specs=pl.BlockSpec(memory_space=pl.ANY),
        out_shape=jax.ShapeDtypeStruct(flux.shape, jnp.float32),
        scratch_shapes=[
            pltpu.SemaphoreType.DMA((1, devices)),
            pltpu.SemaphoreType.DMA((1, devices)),
            pltpu.SemaphoreType.DMA((1,)),
        ],
        compiler_params=pltpu.CompilerParams(collective_id=1, has_side_effects=True),
    )(flux)


def local_blocks(
    wave_now,
    wave_prev,
    potential,
    angular_dvr,
    kinetic_radial,
    kinetic_bond,
    kinetic_third,
    inv_moment,
    rot_level,
    helicity,
    coriolis,
    ladder,
    damping,
    strip_bond,
    strip_third,
    strip_weight,
    strip_length,
    strip_owner,
    strip_cell,
):
    blocks, _, bond_pts, thirds, angles = wave_now.shape
    devices = lax.axis_size("slab")
    cells = bond_pts * thirds
    points = strip_bond.shape[1]
    cuts = devices // blocks
    width = angles // cuts
    high_prec = lax.Precision.HIGH
    wave = wave_now.reshape(blocks, cells, angles)

    live = jnp.arange(points, dtype=jnp.int32)[None, :] < strip_length[:, None]
    weights = jnp.where(live[:, :, None], strip_weight, 0.0)[0].T
    base = (strip_bond * thirds + strip_third).astype(jnp.float32)
    target = (strip_owner[:, :, 0] * P_DEV + strip_cell).astype(jnp.float32)
    table = jnp.concatenate([base, target, weights, jnp.zeros((2, points), jnp.float32)], axis=0)
    field, info = spread(wave, table)

    mixed = jnp.einsum("ij,jca->ica", kinetic_radial, field, precision=high_prec)
    cell_iota = jnp.arange(cells, dtype=jnp.float32)[None, None, :]
    stencil = sum(
        jnp.where(cell_iota == info[:, 0, :, None] + float(t * thirds), info[:, 2 + t, :, None], 0.0)
        for t in range(4)
    )
    surface = jnp.einsum("qpc,qca->qpa", stencil, field, precision=high_prec)
    product_iota = jnp.arange(devices * P_DEV, dtype=jnp.float32)[:, None]
    landing = (product_iota == info[:, 1, :].reshape(-1)[None, :]).astype(jnp.bfloat16)
    flux = split_dot(landing, surface.reshape(devices * points, width))
    back = lax.all_to_all(mixed, "slab", split_axis=0, concat_axis=0, tiled=True)
    flux = send_back(flux.reshape(devices, P_DEV, width))

    kinetic = (
        kinetic_bond[:, None, :, None] * jnp.eye(thirds, dtype=jnp.float32)[None, :, None, :]
        + jnp.eye(bond_pts, dtype=jnp.float32)[:, None, :, None] * kinetic_third[None, :, None, :]
    ).reshape(cells, cells)
    kinetic_term = jnp.einsum("cd,kda->kca", kinetic, wave, precision=high_prec)
    grid_wave = jnp.einsum("kcb,ba->kca", wave, angular_dvr, precision=high_prec)
    potential_term = jnp.einsum(
        "kca,ba->kcb",
        potential.reshape(1, cells, angles) * grid_wave,
        angular_dvr,
        precision=high_prec,
    )
    moment = inv_moment[0]
    rotation_term = moment * (rot_level[None, None, :] + helicity[:, None, None]) * wave
    padding = jnp.zeros((1,) + wave.shape[1:], jnp.float32)
    couple = coriolis[:, None, None]
    above = jnp.concatenate([wave[1:] * couple, padding], axis=0)
    below = jnp.concatenate([padding, wave[:-1] * couple], axis=0)
    coriolis_term = moment * ladder[None, None, :] * (above + below)
    own = kinetic_term + potential_term + rotation_term + coriolis_term
    wave_next, surface_flux = finish(
        back, flux, own, wave_prev.reshape(wave.shape), damping.reshape(cells, 1)
    )
    return wave_next.reshape(wave_now.shape), surface_flux


def plan(*args):
    blocks, local_rows, _, _, angles = args[0].shape
    devices = lax.axis_size("slab")
    cuts = devices // blocks
    fits = (
        local_rows == 1
        and devices % blocks == 0
        and angles % max(cuts, 1) == 0
        and angles // max(cuts, 1) == args[13].shape[1]
        and cuts % 2 == 0
    )
    return local_blocks(*args) if fits else local(*args)


def solution(mesh):
    in_specs = (
        P("groups", "slab", None, None, None),
        P("groups", "slab", None, None, None),
        P("slab", None, None, None),
        P(),
        P(),
        P(),
        P(),
        P("slab"),
        P(),
        P(),
        P(),
        P(),
        P("slab", None, None),
        P("slab", None),
        P("slab", None),
        P("slab", None, None),
        P("slab"),
        P("slab", None, None),
        P("slab", None),
    )
    out_specs = (P("groups", "slab", None, None, None), P("groups", "slab", None))
    return jax.shard_map(plan, mesh=mesh, in_specs=in_specs, out_specs=out_specs, check_vma=False)
```

```python
import functools

import jax
import jax.numpy as jnp
from jax import lax
from jax.experimental import pallas as pl
from jax.experimental.pallas import tpu as pltpu
from jax.sharding import PartitionSpec as P

SMAX = 128
P_DEV = 64


exact_prec = lax.Precision.HIGHEST


def hamiltonian_apply(
    wave,
    radial_term,
    potential,
    angular_dvr,
    kinetic_bond,
    kinetic_third,
    inv_moment,
    rot_level,
    helicity,
    coriolis,
    ladder,
):
    bond_term = jnp.einsum("ij,kqjza->kqiza", kinetic_bond, wave, precision=exact_prec)
    third_term = jnp.einsum("ij,kqrja->kqria", kinetic_third, wave, precision=exact_prec)
    grid_wave = jnp.einsum("kqrzb,ba->kqrza", wave, angular_dvr, precision=exact_prec)
    potential_term = jnp.einsum(
        "kqrza,ba->kqrzb", potential[None] * grid_wave, angular_dvr, precision=exact_prec
    )
    moment = inv_moment[None, :, None, None, None]
    rotation_term = (
        moment * (rot_level[None, None, None, None, :] + helicity[:, None, None, None, None]) * wave
    )
    padding = jnp.zeros((1,) + wave.shape[1:], jnp.float32)
    couple = coriolis[:, None, None, None, None]
    above = jnp.concatenate([wave[1:] * couple, padding], axis=0)
    below = jnp.concatenate([padding, wave[:-1] * couple], axis=0)
    coriolis_term = moment * ladder[None, None, None, None, :] * (above + below)
    return radial_term + bond_term + third_term + potential_term + rotation_term + coriolis_term


def local(
    wave_now,
    wave_prev,
    potential,
    angular_dvr,
    kinetic_radial,
    kinetic_bond,
    kinetic_third,
    inv_moment,
    rot_level,
    helicity,
    coriolis,
    ladder,
    damping,
    strip_bond,
    strip_third,
    strip_weight,
    strip_length,
    strip_owner,
    strip_cell,
):
    blocks, local_rows, bond_pts, thirds, angles = wave_now.shape
    flat_wave = wave_now.reshape(blocks, local_rows, bond_pts * thirds, angles)
    mixed = jnp.einsum(
        "ij,kjca->kica",
        kinetic_radial,
        lax.all_to_all(flat_wave, "slab", split_axis=2, concat_axis=1, tiled=True),
        precision=exact_prec,
    )
    radial_term = lax.all_to_all(mixed, "slab", split_axis=1, concat_axis=2, tiled=True).reshape(
        wave_now.shape
    )
    devices = lax.axis_size("slab")
    slot_count = max(2, 2 * SMAX // devices)
    points = local_rows * SMAX
    cells = wave_now.reshape(blocks, local_rows * bond_pts * thirds, angles)
    stencil_step = jnp.arange(4, dtype=jnp.int32)
    offset = jnp.arange(local_rows, dtype=jnp.int32)[:, None, None] * (bond_pts * thirds)
    cell_idx = (
        offset
        + (strip_bond[:, :, None] + stencil_step[None, None, :]) * thirds
        + strip_third[:, :, None]
    )
    stencil = jnp.take(cells, cell_idx.reshape(-1), axis=1).reshape(blocks, points, 4, angles)
    weights = strip_weight.reshape(points, 4)
    surface = jnp.einsum("pt,kpta->kpa", weights, stencil, precision=exact_prec)
    alive_mask = (
        (jnp.arange(SMAX, dtype=jnp.int32)[None, :] < strip_length[:, None])
        .reshape(points)
        .astype(jnp.float32)
    )
    surface = surface * alive_mask[None, :, None]
    owner = strip_owner.reshape(points)
    onehot = (owner[:, None] == jnp.arange(devices, dtype=jnp.int32)[None, :]).astype(jnp.float32)
    point_iota = jnp.arange(points, dtype=jnp.int32)
    earlier = (point_iota[None, :] < point_iota[:, None]).astype(jnp.float32)
    before = jnp.dot(earlier, onehot, precision=exact_prec)
    order_in = jnp.sum(onehot * before, axis=1).astype(jnp.int32)
    slot_idx = owner * slot_count + order_in
    select = (
        slot_idx[None, :] == jnp.arange(devices * slot_count, dtype=jnp.int32)[:, None]
    ).astype(jnp.float32)
    values = jnp.einsum("qp,kpa->qka", select, surface, precision=exact_prec).reshape(
        devices, slot_count, blocks, angles
    )
    cell_ids = jnp.dot(
        select, strip_cell.reshape(points).astype(jnp.float32), precision=exact_prec
    ).reshape(devices, slot_count)
    got_values, got_cells = (
        lax.all_to_all(values, "slab", split_axis=0, concat_axis=0, tiled=True),
        lax.all_to_all(cell_ids, "slab", split_axis=0, concat_axis=0, tiled=True),
    )
    landing = (
        got_cells.reshape(-1)[None, :] == jnp.arange(P_DEV, dtype=jnp.float32)[:, None]
    ).astype(jnp.float32)
    surface_flux = jnp.einsum(
        "cq,qka->kca",
        landing,
        got_values.reshape(devices * slot_count, blocks, angles),
        precision=exact_prec,
    )
    hamiltonian = hamiltonian_apply(
        wave_now,
        radial_term,
        potential,
        angular_dvr,
        kinetic_bond,
        kinetic_third,
        inv_moment,
        rot_level,
        helicity,
        coriolis,
        ladder,
    )
    damp = damping[None, :, :, :, None]
    wave_next = damp * (0.5 * hamiltonian - damp * wave_prev)
    return (wave_next, surface_flux)


def split_dot(onehot, values):
    high = lax.reduce_precision(values, exponent_bits=8, mantissa_bits=7)
    both = jnp.concatenate([high, values - high], axis=-1).astype(jnp.bfloat16)
    out = jnp.dot(onehot, both, preferred_element_type=jnp.float32)
    width = values.shape[-1]
    return out[:, :width] + out[:, width:]


def finish_kernel(back_ref, own_ref, prev_ref, damp_ref, next_ref, flux_ref):
    cells = own_ref.shape[1]
    cuts = back_ref.shape[0]
    width = back_ref.shape[2]
    damp = damp_ref[...]
    for cut in range(cuts):
        lanes = slice(cut * width, (cut + 1) * width)
        total = back_ref[cut, :cells, :] + own_ref[0, :, lanes]
        next_ref[0, :, lanes] = damp * (0.5 * total - damp * prev_ref[0, :, lanes])
        flux_ref[0, :, lanes] = back_ref[cut, cells:, :]


def finish(back, own, prev, damp):
    blocks, cells, angles = own.shape
    devices, rows, width = back.shape
    parts = 2
    cuts = devices // blocks // parts
    whole = pl.BlockSpec((1, cells, cuts * width), lambda k, h: (k, 0, h))
    return pl.pallas_call(
        finish_kernel,
        grid=(blocks, parts),
        in_specs=[
            pl.BlockSpec((cuts, rows, width), lambda k, h: (k * parts + h, 0, 0)),
            whole,
            whole,
            pl.BlockSpec((cells, 1), lambda k, h: (0, 0)),
        ],
        out_specs=[
            whole,
            pl.BlockSpec((1, rows - cells, cuts * width), lambda k, h: (k, 0, h)),
        ],
        out_shape=[
            jax.ShapeDtypeStruct((blocks, cells, angles), jnp.float32),
            jax.ShapeDtypeStruct((blocks, rows - cells, angles), jnp.float32),
        ],
    )(back, own, prev, damp)


def spread_kernel(devices, wave_ref, table_ref, field_ref, info_ref, send_sem, recv_sem, own_sem):
    blocks, _, angles = wave_ref.shape
    cuts = devices // blocks
    width = angles // cuts
    me = lax.axis_index("slab")
    barrier = pltpu.get_barrier_semaphore()
    for step in range(1, devices):
        pl.semaphore_signal(
            barrier,
            inc=1,
            device_id={"slab": lax.rem(me + step, devices)},
            device_id_type=pl.DeviceIdType.MESH,
        )

    def block(peer):
        lane = pl.multiple_of(lax.rem(peer, cuts) * width, width)
        return wave_ref.at[peer // cuts, :, pl.ds(lane, width)]

    own = [
        pltpu.make_async_copy(block(me), field_ref.at[me], own_sem.at[0]),
        pltpu.make_async_copy(table_ref, info_ref.at[me], own_sem.at[1]),
    ]
    for copy in own:
        copy.start()
    pl.semaphore_wait(barrier, devices - 1)

    ranked = sorted(range(1, devices), key=lambda step: abs(step - devices // 2))
    middle = len(ranked) // 2
    steps = [step for pair in zip(ranked[:middle], ranked[::-1]) for step in pair]
    steps = steps + [step for step in ranked if step not in steps]
    copies = []
    for step in steps:
        peer = lax.rem(me + step, devices)
        pairs = ((block(peer), field_ref.at[me]), (table_ref, info_ref.at[me]))
        for part, (source, target) in enumerate(pairs):
            copy = pltpu.make_async_remote_copy(
                src_ref=source,
                dst_ref=target,
                send_sem=send_sem.at[part, step],
                recv_sem=recv_sem.at[part, step],
                device_id={"slab": peer},
                device_id_type=pl.DeviceIdType.MESH,
            )
            copy.start()
            copies.append(copy)
    for copy in own:
        copy.wait()
    for step in steps:
        sender = lax.rem(me + devices - step, devices)
        pairs = ((block(me), field_ref.at[sender]), (table_ref, info_ref.at[sender]))
        for part, (source, target) in enumerate(pairs):
            pltpu.make_async_remote_copy(
                src_ref=source,
                dst_ref=target,
                send_sem=send_sem.at[part, step],
                recv_sem=recv_sem.at[part, step],
                device_id={"slab": sender},
                device_id_type=pl.DeviceIdType.MESH,
            ).wait_recv()
    for copy in copies:
        copy.wait_send()


def spread(wave, table):
    blocks, cells, angles = wave.shape
    devices = lax.axis_size("slab")
    width = angles // (devices // blocks)
    return pl.pallas_call(
        functools.partial(spread_kernel, devices),
        in_specs=[pl.BlockSpec(memory_space=pl.ANY)] * 2,
        out_specs=[pl.BlockSpec(memory_space=pl.ANY)] * 2,
        out_shape=[
            jax.ShapeDtypeStruct((devices, cells, width), jnp.float32),
            jax.ShapeDtypeStruct((devices,) + table.shape, jnp.float32),
        ],
        scratch_shapes=[
            pltpu.SemaphoreType.DMA((2, devices)),
            pltpu.SemaphoreType.DMA((2, devices)),
            pltpu.SemaphoreType.DMA((2,)),
        ],
        compiler_params=pltpu.CompilerParams(collective_id=0, has_side_effects=True),
    )(wave, table)


def local_blocks(
    wave_now,
    wave_prev,
    potential,
    angular_dvr,
    kinetic_radial,
    kinetic_bond,
    kinetic_third,
    inv_moment,
    rot_level,
    helicity,
    coriolis,
    ladder,
    damping,
    strip_bond,
    strip_third,
    strip_weight,
    strip_length,
    strip_owner,
    strip_cell,
):
    blocks, _, bond_pts, thirds, angles = wave_now.shape
    devices = lax.axis_size("slab")
    cells = bond_pts * thirds
    points = strip_bond.shape[1]
    cuts = devices // blocks
    width = angles // cuts
    high_prec = lax.Precision.HIGH
    wave = wave_now.reshape(blocks, cells, angles)

    live = jnp.arange(points, dtype=jnp.int32)[None, :] < strip_length[:, None]
    weights = jnp.where(live[:, :, None], strip_weight, 0.0)[0].T
    base = (strip_bond * thirds + strip_third).astype(jnp.float32)
    target = (strip_owner[:, :, 0] * P_DEV + strip_cell).astype(jnp.float32)
    table = jnp.concatenate([base, target, weights, jnp.zeros((2, points), jnp.float32)], axis=0)
    field, info = spread(wave, table)

    mixed = jnp.einsum("ij,jca->ica", kinetic_radial, field, precision=high_prec)
    cell_iota = jnp.arange(cells, dtype=jnp.float32)[None, None, :]
    stencil = sum(
        jnp.where(cell_iota == info[:, 0, :, None] + float(t * thirds), info[:, 2 + t, :, None], 0.0)
        for t in range(4)
    )
    surface = jnp.einsum("qpc,qca->qpa", stencil, field, precision=high_prec)
    product_iota = jnp.arange(devices * P_DEV, dtype=jnp.float32)[:, None]
    landing = (product_iota == info[:, 1, :].reshape(-1)[None, :]).astype(jnp.bfloat16)
    flux = split_dot(landing, surface.reshape(devices * points, width))
    back = jnp.concatenate([mixed, flux.reshape(devices, P_DEV, width)], axis=1)
    back = lax.all_to_all(back, "slab", split_axis=0, concat_axis=0, tiled=True)

    kinetic = (
        kinetic_bond[:, None, :, None] * jnp.eye(thirds, dtype=jnp.float32)[None, :, None, :]
        + jnp.eye(bond_pts, dtype=jnp.float32)[:, None, :, None] * kinetic_third[None, :, None, :]
    ).reshape(cells, cells)
    kinetic_term = jnp.einsum("cd,kda->kca", kinetic, wave, precision=high_prec)
    grid_wave = jnp.einsum("kcb,ba->kca", wave, angular_dvr, precision=high_prec)
    potential_term = jnp.einsum(
        "kca,ba->kcb",
        potential.reshape(1, cells, angles) * grid_wave,
        angular_dvr,
        precision=high_prec,
    )
    moment = inv_moment[0]
    rotation_term = moment * (rot_level[None, None, :] + helicity[:, None, None]) * wave
    padding = jnp.zeros((1,) + wave.shape[1:], jnp.float32)
    couple = coriolis[:, None, None]
    above = jnp.concatenate([wave[1:] * couple, padding], axis=0)
    below = jnp.concatenate([padding, wave[:-1] * couple], axis=0)
    coriolis_term = moment * ladder[None, None, :] * (above + below)
    own = kinetic_term + potential_term + rotation_term + coriolis_term
    wave_next, surface_flux = finish(
        back, own, wave_prev.reshape(wave.shape), damping.reshape(cells, 1)
    )
    return wave_next.reshape(wave_now.shape), surface_flux


def plan(*args):
    blocks, local_rows, _, _, angles = args[0].shape
    devices = lax.axis_size("slab")
    cuts = devices // blocks
    fits = (
        local_rows == 1
        and devices % blocks == 0
        and angles % max(cuts, 1) == 0
        and angles // max(cuts, 1) == args[13].shape[1]
        and cuts % 2 == 0
    )
    return local_blocks(*args) if fits else local(*args)


def solution(mesh):
    in_specs = (
        P("groups", "slab", None, None, None),
        P("groups", "slab", None, None, None),
        P("slab", None, None, None),
        P(),
        P(),
        P(),
        P(),
        P("slab"),
        P(),
        P(),
        P(),
        P(),
        P("slab", None, None),
        P("slab", None),
        P("slab", None),
        P("slab", None, None),
        P("slab"),
        P("slab", None, None),
        P("slab", None),
    )
    out_specs = (P("groups", "slab", None, None, None), P("groups", "slab", None))
    return jax.shard_map(plan, mesh=mesh, in_specs=in_specs, out_specs=out_specs, check_vma=False)
```
